256 devices in a mesh: fib: 8 (over y, x_hi), rest: 32 (over z, x_lo, core).
Axes of the slice: x: 4 (x_hi: 2, x_lo: 2; x = x_hi * 2 + x_lo), y: 4, z: 8, core: 2. Of those that a mesh axis runs over, the one named last changes fastest.
Arguments:
- tensor: float32 [64, 128, 64, 1024], P('fib', 'rest'), may hold values from -24 to 24
- factor_one: float32 [1024, 128], replicated, may hold values from 0 to 0.05
- factor_two: float32 [64, 128], P('fib'), may hold values from 0.05 to 0.35
- factor_three: float32 [128, 128], P('rest'), may hold values from 0.03 to 0.25
- factor_four: float32 [64, 128], replicated, may hold values from 0.03 to 0.25
Outputs:
- new_factor: float32 [1024, 128], replicated
- factor_gram: float32 [128, 128], replicated
The draws below stay inside these ranges and needn't reach their ends.
All inputs are finite; a program needn't handle non-finite values.
Results may differ from the reference program's by a relative error of at most 0.00014.
Values sent between devices are 32-bit elements; how exact they have to be, the bound alone decides.
No kernel may reach another device: no remote copies, remote signals or barrier semaphores. Data moves between devices by JAX's collectives and lax.ppermute only.
A program may use at most 64 MiB of HBM per device.

```python
import jax
import jax.numpy as jnp
from jax import lax

RANK = 128
MODE1 = 1024
MODE4 = 64
MODE2 = 64
MODE3 = 128


def strengthened(values, own_key, source, target, shards_of, factor):
    def block_of(position):
        return (jnp.arange(values.shape[position]) // (values.shape[position] // shards_of)).reshape((-1,) + (1,) * (values.ndim - 1 - position))

    near = jax.random.permutation(own_key, shards_of)[block_of(target)]
    second = (block_of(target) + shards_of // 2) % shards_of
    return jnp.where((block_of(source) == near) | (block_of(source) == second), factor * values, values)


def levels(stream_key, shape, pieces, low, top_value):
    factor_of = 1.0
    for position, blocks in pieces:
        heights = jax.random.uniform(jax.random.fold_in(jax.random.fold_in(stream_key, 6), position), (blocks,), jnp.float32, low / len(pieces), top_value / len(pieces))
        factor_of = factor_of * jnp.repeat(jnp.exp(heights), shape[position] // blocks).reshape((-1,) + (1,) * (len(shape) - 1 - position))
    return factor_of


def gaussian_with(stream_key, extent, spread, reach, shards, heavy, dtype=jnp.bfloat16):
    entries = spread * jax.random.normal(stream_key, extent, jnp.float32)
    if shards:
        entries = entries * levels(stream_key, extent, shards, -0.22, 0.18)
    return jnp.clip(strengthened(entries, jax.random.fold_in(stream_key, 3), *heavy), -reach, reach).astype(dtype)


def setup_inputs(seed: int = 0) -> dict:
    streams_of = jax.random.split(jax.random.key(seed), 6)
    return {
        "tensor": gaussian_with(streams_of[0], (MODE2, MODE3, MODE4, MODE1), 4.0, 24.0, ((0, 8), (1, 32)), (1, 3, 32, 2.75), jnp.float32),
        "factor_one": jnp.clip(jax.random.uniform(streams_of[1], (MODE1, RANK), jnp.float32, 0.0, 0.05), 0.0, 0.05),
        "factor_two": jnp.clip(0.05 + 0.29999999 * jax.random.uniform(streams_of[2], (MODE2, RANK), jnp.float32) ** levels(streams_of[2], (MODE2, RANK), ((0, 8),), -0.2, 0.2), 0.05, 0.35),
        "factor_three": jnp.clip(0.03 + 0.22 * jax.random.uniform(streams_of[3], (MODE3, RANK), jnp.float32) ** levels(streams_of[3], (MODE3, RANK), ((0, 32),), -0.2, 0.2), 0.03, 0.25),
        "factor_four": jnp.clip(jax.random.uniform(streams_of[4], (MODE4, RANK), jnp.float32, 0.03, 0.25), 0.03, 0.25),
    }


def hals_columns(factor, mttkrp, gram_v):
    highest = lax.Precision.HIGHEST
    rank_cols = factor.shape[1]
    width = 16 if rank_cols % 16 == 0 else rank_cols
    current = factor
    for block_idx in range(rank_cols // width):
        lower = block_idx * width
        base = jnp.dot(current, gram_v[:, lower:lower + width], precision=highest)
        old_cols = current[:, lower:lower + width]
        inner = gram_v[lower:lower + width, lower:lower + width]
        target = mttkrp[:, lower:lower + width]

        def update(k, cols):
            index = k.astype(jnp.int32)
            zero = jnp.zeros((), jnp.int32)
            inner_col = lax.dynamic_slice_in_dim(inner, index, 1, 1)
            diag = lax.dynamic_slice_in_dim(inner_col, index, 1, 0)[0, 0]
            product = lax.dynamic_slice_in_dim(base, index, 1, 1)[:, 0] + jnp.dot(cols - old_cols, inner_col, precision=highest)[:, 0]
            goal = lax.dynamic_slice_in_dim(target, index, 1, 1)[:, 0]
            column = lax.dynamic_slice_in_dim(cols, index, 1, 1)[:, 0]
            fresh = jnp.maximum(column + (goal - product) / diag, 0.0)
            return lax.dynamic_update_slice(cols, fresh[:, None], (zero, index))

        cols = lax.fori_loop(0, width, update, old_cols)
        current = current.at[:, lower:lower + width].set(cols)
    return current


def reference(tensor, factor_one, factor_two, factor_three, factor_four):
    highest = lax.Precision.HIGHEST

    def accumulate(total, pair):
        block, row_two = pair
        khatri = (row_two[None, None, :] * factor_three[:, None, :] * factor_four[None, :, :]).reshape(-1, RANK)
        flat = block.reshape(-1, MODE1)
        part = lax.dot_general(flat, khatri, (((0,), (0,)), ((), ())), precision=highest)
        return total + part, None

    mttkrp, _ = lax.scan(accumulate, jnp.zeros((MODE1, RANK), jnp.float32), (tensor, factor_two))
    gram_two = jnp.dot(factor_two.T, factor_two, precision=highest)
    gram_three = jnp.dot(factor_three.T, factor_three, precision=highest)
    gram_four = jnp.dot(factor_four.T, factor_four, precision=highest)
    gram_v = gram_two * gram_three * gram_four
    new_factor = hals_columns(factor_one, mttkrp, gram_v)
    factor_gram = jnp.dot(new_factor.T, new_factor, precision=highest)
    return new_factor, factor_gram
```

```python
import jax
import jax.numpy as jnp
from jax import lax
from jax.experimental import pallas as pl
from jax.sharding import Mesh, PartitionSpec as P

HIGHEST = lax.Precision.HIGHEST
PLANE = ("y", "xh", "xl")


def transposed_dot(a, b):
    return lax.dot_general(
        a, b, (((0,), (0,)), ((), ())), precision=HIGHEST, preferred_element_type=jnp.float32
    )


def hals_kernel(parts_ref, two_ref, four_ref, old_ref, out_ref):
    rank = old_ref.shape[1]
    rows = old_ref.shape[0]
    mttkrp = parts_ref[0, :rows, :]
    for z in range(1, parts_ref.shape[0]):
        mttkrp = mttkrp + parts_ref[z, :rows, :]
    three = parts_ref[:, rows:, :].reshape(-1, rank)
    two = two_ref[...]
    four = four_ref[...]
    gram = transposed_dot(two, two) * transposed_dot(three, three) * transposed_dot(four, four)
    row = lax.broadcasted_iota(jnp.int32, (rank, rank), 0)
    col = lax.broadcasted_iota(jnp.int32, (rank, rank), 1)
    diag = jnp.where(row == col, gram, 0.0)
    scale_lane = 1.0 / jnp.sum(diag, axis=0, keepdims=True)
    scale_sub = 1.0 / jnp.sum(diag, axis=1, keepdims=True)
    later = jnp.where(row > col, gram, 0.0)
    rest = (
        mttkrp
        - jnp.dot(old_ref[...], later, precision=HIGHEST, preferred_element_type=jnp.float32)
    ) * scale_lane
    earlier = later * scale_sub
    flipped = jnp.concatenate([rest, jnp.zeros((rank - rows, rank), jnp.float32)], axis=0).T
    tiles = rank // 8
    cols = [flipped[8 * j : 8 * j + 8, :] for j in range(tiles)]
    coef = [earlier[8 * j : 8 * j + 8, :] for j in range(tiles)]
    for k in range(rank):
        tile, sub = divmod(k, 8)
        fresh = jnp.broadcast_to(jnp.maximum(cols[tile], 0.0)[sub : sub + 1, :], (8, rank))
        for j in range(tile if sub < 7 else tile + 1, tiles):
            cols[j] = cols[j] - jnp.broadcast_to(coef[j][:, k : k + 1], (8, rank)) * fresh
    new = jnp.maximum(jnp.concatenate(cols, axis=0), 0.0).T[:rows, :]
    out_ref[...] = jnp.broadcast_to(new[None], out_ref.shape)


def per_device(tensor, factor_one, factor_two, factor_three, factor_four):
    rank = factor_one.shape[1]
    mode_one = tensor.shape[3]
    cores = lax.axis_size("c")
    plane = lax.axis_size(PLANE)
    depth = lax.axis_size("z")
    half = mode_one // cores
    rows = half // plane
    core = lax.axis_index("c")
    plane_pos = lax.axis_index(PLANE)
    khatri = (
        factor_two[:, None, None, :]
        * factor_three[None, :, None, :]
        * factor_four[None, None, :, :]
    ).reshape(-1, rank)
    flat = tensor.reshape(-1, mode_one)
    partial = lax.dot_general(flat, khatri, (((0,), (0,)), ((), ())), precision=HIGHEST)
    partial = partial.reshape(cores, half, rank)
    swap = [(0, 1), (1, 0)]
    other = lax.ppermute(
        jnp.concatenate([lax.dynamic_index_in_dim(partial, 1 - core, 0, False), factor_three, factor_three], axis=0),
        "c",
        swap,
    )
    mine = lax.dynamic_index_in_dim(partial, core, 0, False) + other[:half]
    pair_three = jnp.concatenate([factor_three, other[half : half + 4]], axis=0)
    xl = lax.axis_index("xl")
    seg = plane_pos // 2
    two_rows = lax.dynamic_slice_in_dim(factor_two, 4 * xl, 4, 0)
    three_row = lax.dynamic_slice_in_dim(pair_three, seg, 1, 0)
    extra = jnp.concatenate([two_rows, three_row, three_row, three_row, three_row], axis=0)
    blocks = jnp.concatenate(
        [mine.reshape(plane, rows, rank), jnp.broadcast_to(extra[None], (plane, 8, rank))], axis=1
    )
    got = lax.all_to_all(blocks, PLANE, 0, 0, tiled=True)
    own = jnp.sum(got[:, :rows], axis=0)
    two = got[:, rows : rows + 4].reshape(-1, rank)
    three = got[:, rows + 4]
    block = jnp.concatenate([own, three], axis=0)
    parts = lax.all_to_all(
        jnp.broadcast_to(block[None], (depth, *block.shape)), "z", 0, 0, tiled=True
    )
    old = lax.dynamic_slice_in_dim(factor_one, core * half + plane_pos * rows, rows, 0)
    spread = pl.pallas_call(
        hals_kernel,
        out_shape=jax.ShapeDtypeStruct((plane, rows, rank), jnp.float32),
        name="hals",
    )(parts, two, factor_four, old)
    mine_new = lax.all_to_all(spread, PLANE, 0, 0, tiled=True).reshape(half, rank)
    other_new = lax.ppermute(mine_new, "c", swap)
    first = jnp.where(core == 0, mine_new, other_new)
    second = jnp.where(core == 0, other_new, mine_new)
    new_factor = jnp.concatenate([first, second], axis=0)
    factor_gram = jnp.dot(new_factor.T, new_factor, precision=HIGHEST)
    return (new_factor, factor_gram)


def solution(mesh):
    fine = Mesh(mesh.devices.reshape(4, 2, 8, 2, 2), ("y", "xh", "z", "xl", "c"))
    fib = ("y", "xh")
    rest = ("z", "xl", "c")
    return jax.shard_map(
        per_device,
        mesh=fine,
        in_specs=(P(fib, rest, None, None), P(), P(fib, None), P(rest, None), P()),
        out_specs=(P(), P()),
        check_vma=False,
    )
```

```python
import jax
import jax.numpy as jnp
from jax import lax
from jax.experimental import pallas as pl
from jax.experimental.pallas import tpu as pltpu
from jax.sharding import Mesh, PartitionSpec as P

HIGHEST = lax.Precision.HIGHEST
PLANE = ("y", "xh", "xl")
IN_VMEM = pl.BlockSpec(memory_space=pltpu.VMEM)
IN_PLACE = pl.BlockSpec(memory_space=pl.ANY)


def in_vmem(value):
    return pltpu.with_memory_space_constraint(value, pltpu.VMEM)


def split(value):
    high = value.astype(jnp.bfloat16)
    low = (value - high.astype(jnp.float32)).astype(jnp.bfloat16)
    return high, low


CHUNKS = 4
IN_FLIGHT = 4


def contract_kernel(
    flat_ref, one_hbm, two_hbm, three_hbm, four_hbm, send_ref, keep_ref, old_ref, gram_ref,
    buf, khatri, two_ref, three_ref, four_ref, sems, small_sems,
):
    depth, width = buf.shape[2:]
    rows = old_ref.shape[0]
    rank = gram_ref.shape[0]
    core = lax.axis_index("c")
    start = core * width + lax.axis_index(PLANE) * rows
    small = [
        pltpu.make_async_copy(source, target, small_sems.at[n])
        for n, (source, target) in enumerate(
            (
                (two_hbm, two_ref),
                (three_hbm, three_ref),
                (four_hbm, four_ref),
                (one_hbm.at[pl.ds(pl.multiple_of(start, rows), rows), :], old_ref),
            )
        )
    ]
    for copy in small[:3]:
        copy.start()
    copies = []
    for part in range(2):
        side = (1 - core) if part == 0 else core
        for q in range(CHUNKS):
            copies.append(
                pltpu.make_async_copy(
                    flat_ref.at[pl.ds(q * depth, depth), pl.ds(pl.multiple_of(side * width, width), width)],
                    buf.at[part, q],
                    sems.at[part, q],
                )
            )
    for copy in copies[:IN_FLIGHT]:
        copy.start()
    small[3].start()
    for copy in small[:3]:
        copy.wait()
    four = four_ref[...]
    pairs = two_ref.shape[0] * three_ref.shape[0]
    for q in range(CHUNKS):
        blocks = []
        for p in range(q * pairs // CHUNKS, (q + 1) * pairs // CHUNKS):
            i, j = divmod(p, three_ref.shape[0])
            blocks.append((two_ref[i : i + 1, :] * three_ref[j : j + 1, :]) * four)
        high, low = split(jnp.concatenate(blocks, axis=0).T)
        khatri[q] = jnp.concatenate([high, low], axis=0)
    gram_ref[...] = transposed_dot(four, four)
    send_ref[width : width + three_ref.shape[0], :] = three_ref[...]
    send_ref[width + three_ref.shape[0] :, :] = jnp.zeros_like(three_ref)
    for part, out_ref in ((0, send_ref), (1, keep_ref)):
        both = jnp.zeros((2 * rank, width), jnp.float32)
        cross = jnp.zeros((rank, width), jnp.float32)
        for q in range(CHUNKS):
            n = part * CHUNKS + q
            copies[n].wait()
            if n + IN_FLIGHT < len(copies):
                copies[n + IN_FLIGHT].start()
            high, low = split(buf[part, q])
            both = both + jnp.dot(khatri[q], high, preferred_element_type=jnp.float32)
            cross = cross + jnp.dot(khatri[q, :rank], low, preferred_element_type=jnp.float32)
        out_ref[:width, :] = (both[:rank] + (both[rank:] + cross)).T
    small[3].wait()


def contract(flat, one, two, three, four, half, rows):
    rank = four.shape[1]
    depth = flat.shape[0] // CHUNKS
    return pl.pallas_call(
        contract_kernel,
        out_shape=(
            pltpu.VMEM((half + 2 * three.shape[0], rank), jnp.float32),
            pltpu.VMEM((half, rank), jnp.float32),
            pltpu.VMEM((rows, rank), jnp.float32),
            pltpu.VMEM((rank, rank), jnp.float32),
        ),
        in_specs=[IN_PLACE] * 5,
        out_specs=(IN_VMEM,) * 4,
        scratch_shapes=[
            pltpu.VMEM((2, CHUNKS, depth, half), jnp.float32),
            pltpu.VMEM((CHUNKS, 2 * rank, depth), jnp.bfloat16),
            pltpu.VMEM(two.shape, jnp.float32),
            pltpu.VMEM(three.shape, jnp.float32),
            pltpu.VMEM(four.shape, jnp.float32),
            pltpu.SemaphoreType.DMA((2, CHUNKS)),
            pltpu.SemaphoreType.DMA((4,)),
        ],
        name="contract",
    )(flat, one, two, three, four)


def own_gram(value):
    rank = value.shape[1]
    high, low = split(value)
    both = lax.dot_general(
        high,
        jnp.concatenate([high, low], axis=1),
        (((0,), (0,)), ((), ())),
        preferred_element_type=jnp.float32,
    )
    cross = both[:, rank:]
    return both[:, :rank] + (cross + cross.T)


def half_gram_kernel(mine_ref, gram_ref):
    gram_ref[...] = own_gram(mine_ref[...])


def half_gram(mine):
    rank = mine.shape[1]
    return pl.pallas_call(
        half_gram_kernel,
        out_shape=pltpu.VMEM((rank, rank), jnp.float32),
        in_specs=[IN_VMEM],
        out_specs=IN_VMEM,
        name="half_gram",
    )(in_vmem(mine))


def finish_kernel(mine_ref, other_ref, part_ref, new_ref, gram_ref):
    core = lax.axis_index("c")
    half = mine_ref.shape[0]
    new_ref[pl.ds(pl.multiple_of(core * half, half), half), :] = mine_ref[...]
    new_ref[pl.ds(pl.multiple_of((1 - core) * half, half), half), :] = other_ref[...]
    gram_ref[...] = part_ref[...] + own_gram(other_ref[...])


def finish(mine, other, part):
    half, rank = mine.shape
    return pl.pallas_call(
        finish_kernel,
        out_shape=(
            jax.ShapeDtypeStruct((2 * half, rank), jnp.float32),
            jax.ShapeDtypeStruct((rank, rank), jnp.float32),
        ),
        in_specs=[IN_VMEM] * 3,
        out_specs=(IN_VMEM, IN_VMEM),
        name="finish",
    )(in_vmem(mine), in_vmem(other), in_vmem(part))


def transposed_dot(a, b):
    return lax.dot_general(
        a, b, (((0,), (0,)), ((), ())), precision=HIGHEST, preferred_element_type=jnp.float32
    )


def hals_kernel(parts_ref, got_ref, gram_ref, old_ref, out_ref):
    rows, rank = old_ref.shape
    mttkrp = parts_ref[0, :rows, :]
    for z in range(1, parts_ref.shape[0]):
        mttkrp = mttkrp + parts_ref[z, :rows, :]
    three = parts_ref[:, rows:, :].reshape(-1, rank)
    two = got_ref[:, rows : rows + 4, :].reshape(-1, rank)
    gram = transposed_dot(two, two) * transposed_dot(three, three) * gram_ref[...]
    row = lax.broadcasted_iota(jnp.int32, (rank, rank), 0)
    col = lax.broadcasted_iota(jnp.int32, (rank, rank), 1)
    diag = jnp.where(row == col, gram, 0.0)
    scale_lane = 1.0 / jnp.sum(diag, axis=0, keepdims=True)
    scale_sub = 1.0 / jnp.sum(diag, axis=1, keepdims=True)
    later = jnp.where(row > col, gram, 0.0)
    rest = (
        mttkrp
        - jnp.dot(old_ref[...], later, precision=HIGHEST, preferred_element_type=jnp.float32)
    ) * scale_lane
    earlier = later * scale_sub
    flipped = jnp.concatenate([rest, jnp.zeros((rank - rows, rank), jnp.float32)], axis=0).T
    tiles = rank // 8
    cols = [flipped[8 * j : 8 * j + 8, :] for j in range(tiles)]
    coef = [earlier[8 * j : 8 * j + 8, :] for j in range(tiles)]
    for k in range(rank):
        tile, sub = divmod(k, 8)
        fresh = jnp.broadcast_to(jnp.maximum(cols[tile], 0.0)[sub : sub + 1, :], (8, rank))
        for j in range(tile if sub < 7 else tile + 1, tiles):
            cols[j] = cols[j] - jnp.broadcast_to(coef[j][:, k : k + 1], (8, rank)) * fresh
    new = jnp.maximum(jnp.concatenate(cols, axis=0), 0.0).T[:rows, :]
    out_ref[...] = jnp.broadcast_to(new[None], out_ref.shape)


def per_device(tensor, factor_one, factor_two, factor_three, factor_four):
    rank = factor_one.shape[1]
    mode_one = tensor.shape[3]
    cores = lax.axis_size("c")
    plane = lax.axis_size(PLANE)
    depth = lax.axis_size("z")
    half = mode_one // cores
    rows = half // plane
    plane_pos = lax.axis_index(PLANE)
    flat = tensor.reshape(-1, mode_one)
    send, keep, old, gram_four = contract(
        flat, factor_one, factor_two, factor_three, factor_four, half, rows
    )
    swap = [(0, 1), (1, 0)]
    other = lax.ppermute(send, "c", swap)
    mine = keep + other[:half]
    pair_three = jnp.concatenate([factor_three, other[half : half + 4]], axis=0)
    xl = lax.axis_index("xl")
    seg = plane_pos // 2
    two_rows = lax.dynamic_slice_in_dim(factor_two, 4 * xl, 4, 0)
    three_row = lax.dynamic_slice_in_dim(pair_three, seg, 1, 0)
    extra = jnp.concatenate([two_rows, three_row, three_row, three_row, three_row], axis=0)
    blocks = jnp.concatenate(
        [mine.reshape(plane, rows, rank), jnp.broadcast_to(extra[None], (plane, 8, rank))], axis=1
    )
    got = lax.all_to_all(blocks, PLANE, 0, 0, tiled=True)
    own = jnp.sum(got[:, :rows], axis=0)
    three = got[:, rows + 4]
    block = jnp.concatenate([own, three], axis=0)
    parts = lax.all_to_all(
        jnp.broadcast_to(block[None], (depth, *block.shape)), "z", 0, 0, tiled=True
    )
    spread = pl.pallas_call(
        hals_kernel,
        out_shape=pltpu.VMEM((plane, rows, rank), jnp.float32),
        in_specs=[IN_VMEM] * 4,
        out_specs=IN_VMEM,
        name="hals",
    )(*(in_vmem(v) for v in (parts, got, gram_four, old)))
    mine_new = lax.all_to_all(spread, PLANE, 0, 0, tiled=True).reshape(half, rank)
    other_new = lax.ppermute(mine_new, "c", swap)
    part_gram = half_gram(mine_new)
    return finish(mine_new, other_new, part_gram)


def solution(mesh):
    fine = Mesh(mesh.devices.reshape(4, 2, 8, 2, 2), ("y", "xh", "z", "xl", "c"))
    fib = ("y", "xh")
    rest = ("z", "xl", "c")
    return jax.shard_map(
        per_device,
        mesh=fine,
        in_specs=(P(fib, rest, None, None), P(), P(fib, None), P(rest, None), P()),
        out_specs=(P(), P()),
        check_vma=False,
    )
```

```python
import jax
import jax.numpy as jnp
from jax import lax
from jax.experimental import pallas as pl
from jax.experimental.pallas import tpu as pltpu
from jax.sharding import Mesh, PartitionSpec as P

HIGHEST = lax.Precision.HIGHEST
PLANE = ("y", "xh", "xl")
IN_VMEM = pl.BlockSpec(memory_space=pltpu.VMEM)
IN_PLACE = pl.BlockSpec(memory_space=pl.ANY)


def in_vmem(value):
    return pltpu.with_memory_space_constraint(value, pltpu.VMEM)


def split(value):
    high = value.astype(jnp.bfloat16)
    low = (value - high.astype(jnp.float32)).astype(jnp.bfloat16)
    return high, low


CHUNKS = 4
IN_FLIGHT = 4


def contract_kernel(
    flat_ref, one_hbm, two_hbm, three_hbm, four_hbm, send_ref, keep_ref, old_ref, gram_ref,
    buf, khatri, two_ref, three_ref, four_ref, sems, small_sems,
):
    depth, width = buf.shape[2:]
    rows = old_ref.shape[0]
    rank = gram_ref.shape[0]
    core = lax.axis_index("c")
    start = core * width + lax.axis_index(PLANE) * rows
    small = [
        pltpu.make_async_copy(source, target, small_sems.at[n])
        for n, (source, target) in enumerate(
            (
                (two_hbm, two_ref),
                (three_hbm, three_ref),
                (four_hbm, four_ref),
                (one_hbm.at[pl.ds(pl.multiple_of(start, rows), rows), :], old_ref),
            )
        )
    ]
    for copy in small[:3]:
        copy.start()
    copies = []
    for part in range(2):
        side = (1 - core) if part == 0 else core
        for q in range(CHUNKS):
            copies.append(
                pltpu.make_async_copy(
                    flat_ref.at[pl.ds(q * depth, depth), pl.ds(pl.multiple_of(side * width, width), width)],
                    buf.at[part, q],
                    sems.at[part, q],
                )
            )
    for copy in copies[:IN_FLIGHT]:
        copy.start()
    small[3].start()
    for copy in small[:3]:
        copy.wait()
    four = four_ref[...]
    pairs = two_ref.shape[0] * three_ref.shape[0]
    for q in range(CHUNKS):
        blocks = []
        for p in range(q * pairs // CHUNKS, (q + 1) * pairs // CHUNKS):
            i, j = divmod(p, three_ref.shape[0])
            blocks.append((two_ref[i : i + 1, :] * three_ref[j : j + 1, :]) * four)
        high, low = split(jnp.concatenate(blocks, axis=0).T)
        khatri[q] = jnp.concatenate([high, low], axis=0)
    gram_ref[...] = transposed_dot(four, four)
    send_ref[width : width + three_ref.shape[0], :] = three_ref[...]
    send_ref[width + three_ref.shape[0] :, :] = jnp.zeros_like(three_ref)
    for part, out_ref in ((0, send_ref), (1, keep_ref)):
        both = jnp.zeros((2 * rank, width), jnp.float32)
        cross = jnp.zeros((rank, width), jnp.float32)
        for q in range(CHUNKS):
            n = part * CHUNKS + q
            copies[n].wait()
            if n + IN_FLIGHT < len(copies):
                copies[n + IN_FLIGHT].start()
            high, low = split(buf[part, q])
            both = both + jnp.dot(khatri[q], high, preferred_element_type=jnp.float32)
            cross = cross + jnp.dot(khatri[q, :rank], low, preferred_element_type=jnp.float32)
        out_ref[:width, :] = (both[:rank] + (both[rank:] + cross)).T
    small[3].wait()


def contract(flat, one, two, three, four, half, rows):
    rank = four.shape[1]
    depth = flat.shape[0] // CHUNKS
    return pl.pallas_call(
        contract_kernel,
        out_shape=(
            pltpu.VMEM((half + 2 * three.shape[0], rank), jnp.float32),
            pltpu.VMEM((half, rank), jnp.float32),
            pltpu.VMEM((rows, rank), jnp.float32),
            pltpu.VMEM((rank, rank), jnp.float32),
        ),
        in_specs=[IN_PLACE] * 5,
        out_specs=(IN_VMEM,) * 4,
        scratch_shapes=[
            pltpu.VMEM((2, CHUNKS, depth, half), jnp.float32),
            pltpu.VMEM((CHUNKS, 2 * rank, depth), jnp.bfloat16),
            pltpu.VMEM(two.shape, jnp.float32),
            pltpu.VMEM(three.shape, jnp.float32),
            pltpu.VMEM(four.shape, jnp.float32),
            pltpu.SemaphoreType.DMA((2, CHUNKS)),
            pltpu.SemaphoreType.DMA((4,)),
        ],
        name="contract",
    )(flat, one, two, three, four)


def own_gram(value):
    rank = value.shape[1]
    high, low = split(value)
    both = lax.dot_general(
        high,
        jnp.concatenate([high, low], axis=1),
        (((0,), (0,)), ((), ())),
        preferred_element_type=jnp.float32,
    )
    cross = both[:, rank:]
    return both[:, :rank] + (cross + cross.T)


def half_gram_kernel(mine_ref, gram_ref):
    gram_ref[...] = own_gram(mine_ref[...])


def half_gram(mine):
    rank = mine.shape[1]
    return pl.pallas_call(
        half_gram_kernel,
        out_shape=pltpu.VMEM((rank, rank), jnp.float32),
        in_specs=[IN_VMEM],
        out_specs=IN_VMEM,
        name="half_gram",
    )(in_vmem(mine))


def finish_kernel(mine_ref, other_ref, part_ref, new_ref, gram_ref):
    core = lax.axis_index("c")
    half = mine_ref.shape[0]
    new_ref[pl.ds(pl.multiple_of(core * half, half), half), :] = mine_ref[...]
    new_ref[pl.ds(pl.multiple_of((1 - core) * half, half), half), :] = other_ref[...]
    gram_ref[...] = part_ref[...] + own_gram(other_ref[...])


def finish(mine, other, part):
    half, rank = mine.shape
    return pl.pallas_call(
        finish_kernel,
        out_shape=(
            jax.ShapeDtypeStruct((2 * half, rank), jnp.float32),
            jax.ShapeDtypeStruct((rank, rank), jnp.float32),
        ),
        in_specs=[IN_VMEM] * 3,
        out_specs=(IN_VMEM, IN_VMEM),
        name="finish",
    )(in_vmem(mine), in_vmem(other), in_vmem(part))


def transposed_dot(a, b):
    return lax.dot_general(
        a, b, (((0,), (0,)), ((), ())), precision=HIGHEST, preferred_element_type=jnp.float32
    )


def hals_kernel(
    pair_ref, after_ref, before_ref, across_ref, got_ref, gram_ref, old_ref, out_ref, three_ref
):
    rows, rank = old_ref.shape
    depth = lax.axis_size("z")
    here = lax.axis_index("z")
    blocks = three_ref.shape[0] // depth
    pairs = ((pair_ref, 0), (across_ref, depth // 2), (after_ref, depth - 2), (before_ref, 2))
    sums = []
    for ref, step in pairs:
        first = lax.rem(here + step, depth)
        second = first + 1 - 2 * lax.rem(first, 2)
        for n, z in enumerate((first, second)):
            three_ref[pl.ds(pl.multiple_of(z * blocks, blocks), blocks), :] = ref[n, rows:, :]
        sums.append(ref[0, :rows, :] + ref[1, :rows, :])
    mttkrp = (sums[0] + sums[1]) + (sums[2] + sums[3])
    three = three_ref[...]
    two = got_ref[:, rows : rows + 4, :].reshape(-1, rank)
    gram = transposed_dot(two, two) * transposed_dot(three, three) * gram_ref[...]
    row = lax.broadcasted_iota(jnp.int32, (rank, rank), 0)
    col = lax.broadcasted_iota(jnp.int32, (rank, rank), 1)
    diag = jnp.where(row == col, gram, 0.0)
    scale_lane = 1.0 / jnp.sum(diag, axis=0, keepdims=True)
    scale_sub = 1.0 / jnp.sum(diag, axis=1, keepdims=True)
    later = jnp.where(row > col, gram, 0.0)
    rest = (
        mttkrp
        - jnp.dot(old_ref[...], later, precision=HIGHEST, preferred_element_type=jnp.float32)
    ) * scale_lane
    earlier = later * scale_sub
    flipped = jnp.concatenate([rest, jnp.zeros((rank - rows, rank), jnp.float32)], axis=0).T
    tiles = rank // 8
    cols = [flipped[8 * j : 8 * j + 8, :] for j in range(tiles)]
    coef = [earlier[8 * j : 8 * j + 8, :] for j in range(tiles)]
    for k in range(rank):
        tile, sub = divmod(k, 8)
        fresh = jnp.broadcast_to(jnp.maximum(cols[tile], 0.0)[sub : sub + 1, :], (8, rank))
        for j in range(tile if sub < 7 else tile + 1, tiles):
            cols[j] = cols[j] - jnp.broadcast_to(coef[j][:, k : k + 1], (8, rank)) * fresh
    new = jnp.maximum(jnp.concatenate(cols, axis=0), 0.0).T[:rows, :]
    out_ref[...] = jnp.broadcast_to(new[None], out_ref.shape)


def per_device(tensor, factor_one, factor_two, factor_three, factor_four):
    rank = factor_one.shape[1]
    mode_one = tensor.shape[3]
    cores = lax.axis_size("c")
    plane = lax.axis_size(PLANE)
    depth = lax.axis_size("z")
    half = mode_one // cores
    rows = half // plane
    plane_pos = lax.axis_index(PLANE)
    flat = tensor.reshape(-1, mode_one)
    send, keep, old, gram_four = contract(
        flat, factor_one, factor_two, factor_three, factor_four, half, rows
    )
    swap = [(0, 1), (1, 0)]
    other = lax.ppermute(send, "c", swap)
    mine = keep + other[:half]
    pair_three = jnp.concatenate([factor_three, other[half : half + 4]], axis=0)
    xl = lax.axis_index("xl")
    seg = plane_pos // 2
    two_rows = lax.dynamic_slice_in_dim(factor_two, 4 * xl, 4, 0)
    three_row = lax.dynamic_slice_in_dim(pair_three, seg, 1, 0)
    extra = jnp.concatenate([two_rows, three_row, three_row, three_row, three_row], axis=0)
    blocks = jnp.concatenate(
        [mine.reshape(plane, rows, rank), jnp.broadcast_to(extra[None], (plane, 8, rank))], axis=1
    )
    got = lax.all_to_all(blocks, PLANE, 0, 0, tiled=True)
    own = jnp.sum(got[:, :rows], axis=0)
    three = got[:, rows + 4]
    block = jnp.concatenate([own, three], axis=0)
    block_rows = three.shape[0]
    pair = jnp.stack([block, lax.ppermute(block, "z", [(i, i ^ 1) for i in range(depth)])])
    after, before, across = (
        lax.ppermute(pair, "z", [(i, (i + step) % depth) for i in range(depth)])
        for step in (2, depth - 2, depth // 2)
    )
    spread = pl.pallas_call(
        hals_kernel,
        out_shape=pltpu.VMEM((plane, rows, rank), jnp.float32),
        in_specs=[IN_VMEM] * 7,
        out_specs=IN_VMEM,
        scratch_shapes=[pltpu.VMEM((depth * block_rows, rank), jnp.float32)],
        name="hals",
    )(*(in_vmem(v) for v in (pair, after, before, across, got, gram_four, old)))
    mine_new = lax.all_to_all(spread, PLANE, 0, 0, tiled=True).reshape(half, rank)
    other_new = lax.ppermute(mine_new, "c", swap)
    part_gram = half_gram(mine_new)
    return finish(mine_new, other_new, part_gram)


def solution(mesh):
    fine = Mesh(mesh.devices.reshape(4, 2, 8, 2, 2), ("y", "xh", "z", "xl", "c"))
    fib = ("y", "xh")
    rest = ("z", "xl", "c")
    return jax.shard_map(
        per_device,
        mesh=fine,
        in_specs=(P(fib, rest, None, None), P(), P(fib, None), P(rest, None), P()),
        out_specs=(P(), P()),
        check_vma=False,
    )
```

```python
import jax
import jax.numpy as jnp
from jax import lax
from jax.experimental import pallas as pl
from jax.experimental.pallas import tpu as pltpu
from jax.sharding import Mesh, PartitionSpec as P

HIGHEST = lax.Precision.HIGHEST
PLANE = ("y", "xh", "xl")
Z_MASKS = (7, 1, 2)
IN_VMEM = pl.BlockSpec(memory_space=pltpu.VMEM)
IN_PLACE = pl.BlockSpec(memory_space=pl.ANY)


def in_vmem(value):
    return pltpu.with_memory_space_constraint(value, pltpu.VMEM)


def split(value):
    high = value.astype(jnp.bfloat16)
    low = (value - high.astype(jnp.float32)).astype(jnp.bfloat16)
    return high, low


CHUNKS = 4
IN_FLIGHT = 4


def contract_kernel(
    flat_ref, one_hbm, two_hbm, three_hbm, four_hbm, send_ref, keep_ref, old_ref, gram_ref,
    buf, khatri, two_ref, three_ref, four_ref, sems, small_sems,
):
    depth, width = buf.shape[2:]
    rows = old_ref.shape[0]
    rank = gram_ref.shape[0]
    core = lax.axis_index("c")
    start = core * width + lax.axis_index(PLANE) * rows
    small = [
        pltpu.make_async_copy(source, target, small_sems.at[n])
        for n, (source, target) in enumerate(
            (
                (two_hbm, two_ref),
                (three_hbm, three_ref),
                (four_hbm, four_ref),
                (one_hbm.at[pl.ds(pl.multiple_of(start, rows), rows), :], old_ref),
            )
        )
    ]
    for copy in small[:3]:
        copy.start()
    copies = []
    for part in range(2):
        side = (1 - core) if part == 0 else core
        for q in range(CHUNKS):
            copies.append(
                pltpu.make_async_copy(
                    flat_ref.at[pl.ds(q * depth, depth), pl.ds(pl.multiple_of(side * width, width), width)],
                    buf.at[part, q],
                    sems.at[part, q],
                )
            )
    for copy in copies[:IN_FLIGHT]:
        copy.start()
    small[3].start()
    for copy in small[:3]:
        copy.wait()
    four = four_ref[...]
    pairs = two_ref.shape[0] * three_ref.shape[0]
    for q in range(CHUNKS):
        blocks = []
        for p in range(q * pairs // CHUNKS, (q + 1) * pairs // CHUNKS):
            i, j = divmod(p, three_ref.shape[0])
            blocks.append((two_ref[i : i + 1, :] * three_ref[j : j + 1, :]) * four)
        high, low = split(jnp.concatenate(blocks, axis=0).T)
        khatri[q] = jnp.concatenate([high, low], axis=0)
    gram_ref[...] = transposed_dot(four, four)
    send_ref[width : width + three_ref.shape[0], :] = three_ref[...]
    send_ref[width + three_ref.shape[0] :, :] = jnp.zeros_like(three_ref)
    for part, out_ref in ((0, send_ref), (1, keep_ref)):
        both = jnp.zeros((2 * rank, width), jnp.float32)
        cross = jnp.zeros((rank, width), jnp.float32)
        for q in range(CHUNKS):
            n = part * CHUNKS + q
            copies[n].wait()
            if n + IN_FLIGHT < len(copies):
                copies[n + IN_FLIGHT].start()
            high, low = split(buf[part, q])
            both = both + jnp.dot(khatri[q], high, preferred_element_type=jnp.float32)
            cross = cross + jnp.dot(khatri[q, :rank], low, preferred_element_type=jnp.float32)
        out_ref[:width, :] = (both[:rank] + (both[rank:] + cross)).T
    small[3].wait()


def contract(flat, one, two, three, four, half, rows):
    rank = four.shape[1]
    depth = flat.shape[0] // CHUNKS
    return pl.pallas_call(
        contract_kernel,
        out_shape=(
            pltpu.VMEM((half + 2 * three.shape[0], rank), jnp.float32),
            pltpu.VMEM((half, rank), jnp.float32),
            pltpu.VMEM((rows, rank), jnp.float32),
            pltpu.VMEM((rank, rank), jnp.float32),
        ),
        in_specs=[IN_PLACE] * 5,
        out_specs=(IN_VMEM,) * 4,
        scratch_shapes=[
            pltpu.VMEM((2, CHUNKS, depth, half), jnp.float32),
            pltpu.VMEM((CHUNKS, 2 * rank, depth), jnp.bfloat16),
            pltpu.VMEM(two.shape, jnp.float32),
            pltpu.VMEM(three.shape, jnp.float32),
            pltpu.VMEM(four.shape, jnp.float32),
            pltpu.SemaphoreType.DMA((2, CHUNKS)),
            pltpu.SemaphoreType.DMA((4,)),
        ],
        name="contract",
    )(flat, one, two, three, four)


def own_gram(value):
    rank = value.shape[1]
    high, low = split(value)
    both = lax.dot_general(
        high,
        jnp.concatenate([high, low], axis=1),
        (((0,), (0,)), ((), ())),
        preferred_element_type=jnp.float32,
    )
    cross = both[:, rank:]
    return both[:, :rank] + (cross + cross.T)


def half_gram_kernel(mine_ref, gram_ref):
    gram_ref[...] = own_gram(mine_ref[...])


def half_gram(mine):
    rank = mine.shape[1]
    return pl.pallas_call(
        half_gram_kernel,
        out_shape=pltpu.VMEM((rank, rank), jnp.float32),
        in_specs=[IN_VMEM],
        out_specs=IN_VMEM,
        name="half_gram",
    )(in_vmem(mine))


def finish_kernel(mine_ref, other_ref, part_ref, new_ref, gram_ref):
    core = lax.axis_index("c")
    half = mine_ref.shape[0]
    new_ref[pl.ds(pl.multiple_of(core * half, half), half), :] = mine_ref[...]
    new_ref[pl.ds(pl.multiple_of((1 - core) * half, half), half), :] = other_ref[...]
    gram_ref[...] = part_ref[...] + own_gram(other_ref[...])


def finish(mine, other, part):
    half, rank = mine.shape
    return pl.pallas_call(
        finish_kernel,
        out_shape=(
            jax.ShapeDtypeStruct((2 * half, rank), jnp.float32),
            jax.ShapeDtypeStruct((rank, rank), jnp.float32),
        ),
        in_specs=[IN_VMEM] * 3,
        out_specs=(IN_VMEM, IN_VMEM),
        name="finish",
    )(in_vmem(mine), in_vmem(other), in_vmem(part))


def transposed_dot(a, b):
    return lax.dot_general(
        a, b, (((0,), (0,)), ((), ())), precision=HIGHEST, preferred_element_type=jnp.float32
    )


def hals_kernel(block_ref, peer_ref, got_ref, gram_ref, old_ref, out_ref, three_ref):
    rows, rank = old_ref.shape
    here = lax.axis_index("z")
    held = [0]
    for mask in Z_MASKS[:-1]:
        held += [mask ^ other for other in held]
    size = (block_ref.shape[0] - rows) // len(held)
    for ref, mask in ((block_ref, 0), (peer_ref, Z_MASKS[-1])):
        for n, other in enumerate(held):
            z = jnp.bitwise_xor(here, mask ^ other)
            three_ref[pl.ds(pl.multiple_of(z * size, size), size), :] = ref[
                rows + n * size : rows + (n + 1) * size, :
            ]
    mttkrp = block_ref[:rows, :] + peer_ref[:rows, :]
    three = three_ref[...]
    two = got_ref[:, rows : rows + 4, :].reshape(-1, rank)
    gram = transposed_dot(two, two) * transposed_dot(three, three) * gram_ref[...]
    row = lax.broadcasted_iota(jnp.int32, (rank, rank), 0)
    col = lax.broadcasted_iota(jnp.int32, (rank, rank), 1)
    diag = jnp.where(row == col, gram, 0.0)
    scale_lane = 1.0 / jnp.sum(diag, axis=0, keepdims=True)
    scale_sub = 1.0 / jnp.sum(diag, axis=1, keepdims=True)
    later = jnp.where(row > col, gram, 0.0)
    rest = (
        mttkrp
        - jnp.dot(old_ref[...], later, precision=HIGHEST, preferred_element_type=jnp.float32)
    ) * scale_lane
    earlier = later * scale_sub
    flipped = jnp.concatenate([rest, jnp.zeros((rank - rows, rank), jnp.float32)], axis=0).T
    tiles = rank // 8
    cols = [flipped[8 * j : 8 * j + 8, :] for j in range(tiles)]
    coef = [earlier[8 * j : 8 * j + 8, :] for j in range(tiles)]
    for k in range(rank):
        tile, sub = divmod(k, 8)
        fresh = jnp.broadcast_to(jnp.maximum(cols[tile], 0.0)[sub : sub + 1, :], (8, rank))
        for j in range(tile if sub < 7 else tile + 1, tiles):
            cols[j] = cols[j] - jnp.broadcast_to(coef[j][:, k : k + 1], (8, rank)) * fresh
    new = jnp.maximum(jnp.concatenate(cols, axis=0), 0.0).T[:rows, :]
    out_ref[...] = jnp.broadcast_to(new[None], out_ref.shape)


def per_device(tensor, factor_one, factor_two, factor_three, factor_four):
    rank = factor_one.shape[1]
    mode_one = tensor.shape[3]
    cores = lax.axis_size("c")
    plane = lax.axis_size(PLANE)
    depth = lax.axis_size("z")
    half = mode_one // cores
    rows = half // plane
    plane_pos = lax.axis_index(PLANE)
    flat = tensor.reshape(-1, mode_one)
    send, keep, old, gram_four = contract(
        flat, factor_one, factor_two, factor_three, factor_four, half, rows
    )
    swap = [(0, 1), (1, 0)]
    other = lax.ppermute(send, "c", swap)
    mine = keep + other[:half]
    pair_three = jnp.concatenate([factor_three, other[half : half + 4]], axis=0)
    xl = lax.axis_index("xl")
    seg = plane_pos // 2
    two_rows = lax.dynamic_slice_in_dim(factor_two, 4 * xl, 4, 0)
    three_row = lax.dynamic_slice_in_dim(pair_three, seg, 1, 0)
    extra = jnp.concatenate([two_rows, three_row, three_row, three_row, three_row], axis=0)
    blocks = jnp.concatenate(
        [mine.reshape(plane, rows, rank), jnp.broadcast_to(extra[None], (plane, 8, rank))], axis=1
    )
    got = lax.all_to_all(blocks, PLANE, 0, 0, tiled=True)
    own = jnp.sum(got[:, :rows], axis=0)
    three = got[:, rows + 4]
    for mask in Z_MASKS:
        block = jnp.concatenate([own, three], axis=0)
        peer = lax.ppermute(block, "z", [(i, i ^ mask) for i in range(depth)])
        if mask != Z_MASKS[-1]:
            own = own + peer[:rows]
            three = jnp.concatenate([three, peer[rows:]], axis=0)
    spread = pl.pallas_call(
        hals_kernel,
        out_shape=pltpu.VMEM((plane, rows, rank), jnp.float32),
        in_specs=[IN_VMEM] * 5,
        out_specs=IN_VMEM,
        scratch_shapes=[pltpu.VMEM((2 * three.shape[0], rank), jnp.float32)],
        name="hals",
    )(*(in_vmem(v) for v in (block, peer, got, gram_four, old)))
    mine_new = lax.all_to_all(spread, PLANE, 0, 0, tiled=True).reshape(half, rank)
    other_new = lax.ppermute(mine_new, "c", swap)
    part_gram = half_gram(mine_new)
    return finish(mine_new, other_new, part_gram)


def solution(mesh):
    fine = Mesh(mesh.devices.reshape(4, 2, 8, 2, 2), ("y", "xh", "z", "xl", "c"))
    fib = ("y", "xh")
    rest = ("z", "xl", "c")
    return jax.shard_map(
        per_device,
        mesh=fine,
        in_specs=(P(fib, rest, None, None), P(), P(fib, None), P(rest, None), P()),
        out_specs=(P(), P()),
        check_vma=False,
    )
```

```python
import jax
import jax.numpy as jnp
from jax import lax
from jax.experimental import pallas as pl
from jax.experimental.pallas import tpu as pltpu
from jax.sharding import Mesh, PartitionSpec as P

HIGHEST = lax.Precision.HIGHEST
PLANE = ("y", "xh", "xl")
Z_MASKS = (1, 2, 7)
IN_VMEM = pl.BlockSpec(memory_space=pltpu.VMEM)
IN_PLACE = pl.BlockSpec(memory_space=pl.ANY)


def in_vmem(value):
    return pltpu.with_memory_space_constraint(value, pltpu.VMEM)


def split(value):
    high = value.astype(jnp.bfloat16)
    low = (value - high.astype(jnp.float32)).astype(jnp.bfloat16)
    return high, low


CHUNKS = 4
IN_FLIGHT = 4


def contract_kernel(
    flat_ref, one_hbm, two_hbm, three_hbm, four_hbm, send_ref, keep_ref, old_ref, gram_ref,
    buf, khatri, two_ref, three_ref, four_ref, sems, small_sems,
):
    depth, width = buf.shape[2:]
    rows = old_ref.shape[0]
    rank = gram_ref.shape[0]
    core = lax.axis_index("c")
    start = core * width + lax.axis_index(PLANE) * rows
    small = [
        pltpu.make_async_copy(source, target, small_sems.at[n])
        for n, (source, target) in enumerate(
            (
                (two_hbm, two_ref),
                (three_hbm, three_ref),
                (four_hbm, four_ref),
                (one_hbm.at[pl.ds(pl.multiple_of(start, rows), rows), :], old_ref),
            )
        )
    ]
    for copy in small[:3]:
        copy.start()
    copies = []
    for part in range(2):
        side = (1 - core) if part == 0 else core
        for q in range(CHUNKS):
            copies.append(
                pltpu.make_async_copy(
                    flat_ref.at[pl.ds(q * depth, depth), pl.ds(pl.multiple_of(side * width, width), width)],
                    buf.at[part, q],
                    sems.at[part, q],
                )
            )
    for copy in copies[:IN_FLIGHT]:
        copy.start()
    small[3].start()
    for copy in small[:3]:
        copy.wait()
    four = four_ref[...]
    pairs = two_ref.shape[0] * three_ref.shape[0]
    for q in range(CHUNKS):
        blocks = []
        for p in range(q * pairs // CHUNKS, (q + 1) * pairs // CHUNKS):
            i, j = divmod(p, three_ref.shape[0])
            blocks.append((two_ref[i : i + 1, :] * three_ref[j : j + 1, :]) * four)
        high, low = split(jnp.concatenate(blocks, axis=0).T)
        khatri[q] = jnp.concatenate([high, low], axis=0)
    gram_ref[...] = transposed_dot(four, four)
    send_ref[width : width + three_ref.shape[0], :] = three_ref[...]
    send_ref[width + three_ref.shape[0] :, :] = jnp.zeros_like(three_ref)
    for part, out_ref in ((0, send_ref), (1, keep_ref)):
        both = jnp.zeros((2 * rank, width), jnp.float32)
        cross = jnp.zeros((rank, width), jnp.float32)
        for q in range(CHUNKS):
            n = part * CHUNKS + q
            copies[n].wait()
            if n + IN_FLIGHT < len(copies):
                copies[n + IN_FLIGHT].start()
            high, low = split(buf[part, q])
            both = both + jnp.dot(khatri[q], high, preferred_element_type=jnp.float32)
            cross = cross + jnp.dot(khatri[q, :rank], low, preferred_element_type=jnp.float32)
        out_ref[:width, :] = (both[:rank] + (both[rank:] + cross)).T
    small[3].wait()


def contract(flat, one, two, three, four, half, rows):
    rank = four.shape[1]
    depth = flat.shape[0] // CHUNKS
    return pl.pallas_call(
        contract_kernel,
        out_shape=(
            pltpu.VMEM((half + 2 * three.shape[0], rank), jnp.float32),
            pltpu.VMEM((half, rank), jnp.float32),
            pltpu.VMEM((rows, rank), jnp.float32),
            pltpu.VMEM((rank, rank), jnp.float32),
        ),
        in_specs=[IN_PLACE] * 5,
        out_specs=(IN_VMEM,) * 4,
        scratch_shapes=[
            pltpu.VMEM((2, CHUNKS, depth, half), jnp.float32),
            pltpu.VMEM((CHUNKS, 2 * rank, depth), jnp.bfloat16),
            pltpu.VMEM(two.shape, jnp.float32),
            pltpu.VMEM(three.shape, jnp.float32),
            pltpu.VMEM(four.shape, jnp.float32),
            pltpu.SemaphoreType.DMA((2, CHUNKS)),
            pltpu.SemaphoreType.DMA((4,)),
        ],
        name="contract",
    )(flat, one, two, three, four)


def own_gram(value):
    rank = value.shape[1]
    high, low = split(value)
    both = lax.dot_general(
        high,
        jnp.concatenate([high, low], axis=1),
        (((0,), (0,)), ((), ())),
        preferred_element_type=jnp.float32,
    )
    cross = both[:, rank:]
    return both[:, :rank] + (cross + cross.T)


def half_gram_kernel(mine_ref, gram_ref):
    gram_ref[...] = own_gram(mine_ref[...])


def half_gram(mine):
    rank = mine.shape[1]
    return pl.pallas_call(
        half_gram_kernel,
        out_shape=pltpu.VMEM((rank, rank), jnp.float32),
        in_specs=[IN_VMEM],
        out_specs=IN_VMEM,
        name="half_gram",
    )(in_vmem(mine))


def finish_kernel(mine_ref, other_ref, part_ref, new_ref, gram_ref):
    core = lax.axis_index("c")
    half = mine_ref.shape[0]
    new_ref[pl.ds(pl.multiple_of(core * half, half), half), :] = mine_ref[...]
    new_ref[pl.ds(pl.multiple_of((1 - core) * half, half), half), :] = other_ref[...]
    gram_ref[...] = part_ref[...] + own_gram(other_ref[...])


def finish(mine, other, part):
    half, rank = mine.shape
    return pl.pallas_call(
        finish_kernel,
        out_shape=(
            jax.ShapeDtypeStruct((2 * half, rank), jnp.float32),
            jax.ShapeDtypeStruct((rank, rank), jnp.float32),
        ),
        in_specs=[IN_VMEM] * 3,
        out_specs=(IN_VMEM, IN_VMEM),
        name="finish",
    )(in_vmem(mine), in_vmem(other), in_vmem(part))


def transposed_dot(a, b):
    return lax.dot_general(
        a, b, (((0,), (0,)), ((), ())), precision=HIGHEST, preferred_element_type=jnp.float32
    )


def hals_kernel(block_ref, peer_ref, got_ref, gram_ref, old_ref, out_ref, three_ref):
    rows, rank = old_ref.shape
    here = lax.axis_index("z")
    held = [0]
    for mask in Z_MASKS[:-1]:
        held += [mask ^ other for other in held]
    size = (block_ref.shape[0] - rows) // len(held)
    for ref, mask in ((block_ref, 0), (peer_ref, Z_MASKS[-1])):
        for n, other in enumerate(held):
            z = jnp.bitwise_xor(here, mask ^ other)
            three_ref[pl.ds(pl.multiple_of(z * size, size), size), :] = ref[
                rows + n * size : rows + (n + 1) * size, :
            ]
    mttkrp = block_ref[:rows, :] + peer_ref[:rows, :]
    three = three_ref[...]
    two = got_ref[:, rows : rows + 4, :].reshape(-1, rank)
    gram = transposed_dot(two, two) * transposed_dot(three, three) * gram_ref[...]
    row = lax.broadcasted_iota(jnp.int32, (rank, rank), 0)
    col = lax.broadcasted_iota(jnp.int32, (rank, rank), 1)
    diag = jnp.where(row == col, gram, 0.0)
    scale_lane = 1.0 / jnp.sum(diag, axis=0, keepdims=True)
    scale_sub = 1.0 / jnp.sum(diag, axis=1, keepdims=True)
    later = jnp.where(row > col, gram, 0.0)
    rest = (
        mttkrp
        - jnp.dot(old_ref[...], later, precision=HIGHEST, preferred_element_type=jnp.float32)
    ) * scale_lane
    earlier = later * scale_sub
    flipped = jnp.concatenate([rest, jnp.zeros((rank - rows, rank), jnp.float32)], axis=0).T
    tiles = rank // 8
    cols = [flipped[8 * j : 8 * j + 8, :] for j in range(tiles)]
    coef = [earlier[8 * j : 8 * j + 8, :] for j in range(tiles)]
    for k in range(rank):
        tile, sub = divmod(k, 8)
        fresh = jnp.broadcast_to(jnp.maximum(cols[tile], 0.0)[sub : sub + 1, :], (8, rank))
        for j in range(tile if sub < 7 else tile + 1, tiles):
            cols[j] = cols[j] - jnp.broadcast_to(coef[j][:, k : k + 1], (8, rank)) * fresh
    new = jnp.maximum(jnp.concatenate(cols, axis=0), 0.0).T[:rows, :]
    out_ref[...] = jnp.broadcast_to(new[None], out_ref.shape)


def per_device(tensor, factor_one, factor_two, factor_three, factor_four):
    rank = factor_one.shape[1]
    mode_one = tensor.shape[3]
    cores = lax.axis_size("c")
    plane = lax.axis_size(PLANE)
    depth = lax.axis_size("z")
    half = mode_one // cores
    rows = half // plane
    plane_pos = lax.axis_index(PLANE)
    flat = tensor.reshape(-1, mode_one)
    send, keep, old, gram_four = contract(
        flat, factor_one, factor_two, factor_three, factor_four, half, rows
    )
    swap = [(0, 1), (1, 0)]
    other = lax.ppermute(send, "c", swap)
    mine = keep + other[:half]
    pair_three = jnp.concatenate([factor_three, other[half : half + 4]], axis=0)
    xl = lax.axis_index("xl")
    seg = plane_pos // 2
    two_rows = lax.dynamic_slice_in_dim(factor_two, 4 * xl, 4, 0)
    three_row = lax.dynamic_slice_in_dim(pair_three, seg, 1, 0)
    extra = jnp.concatenate([two_rows, three_row, three_row, three_row, three_row], axis=0)
    blocks = jnp.concatenate(
        [mine.reshape(plane, rows, rank), jnp.broadcast_to(extra[None], (plane, 8, rank))], axis=1
    )
    got = lax.all_to_all(blocks, PLANE, 0, 0, tiled=True)
    own = jnp.sum(got[:, :rows], axis=0)
    three = got[:, rows + 4]
    for mask in Z_MASKS:
        block = jnp.concatenate([own, three], axis=0)
        peer = lax.ppermute(block, "z", [(i, i ^ mask) for i in range(depth)])
        if mask != Z_MASKS[-1]:
            own = own + peer[:rows]
            three = jnp.concatenate([three, peer[rows:]], axis=0)
    spread = pl.pallas_call(
        hals_kernel,
        out_shape=pltpu.VMEM((plane, rows, rank), jnp.float32),
        in_specs=[IN_VMEM] * 5,
        out_specs=IN_VMEM,
        scratch_shapes=[pltpu.VMEM((2 * three.shape[0], rank), jnp.float32)],
        name="hals",
    )(*(in_vmem(v) for v in (block, peer, got, gram_four, old)))
    mine_new = lax.all_to_all(spread, PLANE, 0, 0, tiled=True).reshape(half, rank)
    other_new = lax.ppermute(mine_new, "c", swap)
    part_gram = half_gram(mine_new)
    return finish(mine_new, other_new, part_gram)


def solution(mesh):
    fine = Mesh(mesh.devices.reshape(4, 2, 8, 2, 2), ("y", "xh", "z", "xl", "c"))
    fib = ("y", "xh")
    rest = ("z", "xl", "c")
    return jax.shard_map(
        per_device,
        mesh=fine,
        in_specs=(P(fib, rest, None, None), P(), P(fib, None), P(rest, None), P()),
        out_specs=(P(), P()),
        check_vma=False,
    )
```
